32 devices in a mesh: gx: 8 (over z, y), gy: 4 (over x, core).
Axes of the slice: x: 2, y: 2, z: 4, core: 2. Of those that a mesh axis runs over, the one named last changes fastest.
Arguments:
- features: bfloat16 [8, 4, 2048, 256], P('gx', 'gy'), may hold values from -6 to 6
- pre_norm: bfloat16 [8, 4, 2048, 256], P('gx', 'gy')
- out_grad: bfloat16 [8, 4, 2048, 256], P('gx', 'gy'), may hold values from -6 to 6
- weight: bfloat16 [27, 256, 256], replicated, may hold values from -0.375 to 0.375
- gamma: float32 [256], replicated, may hold values from 0.1 to 1.9
- beta: float32 [256], replicated, may hold values from -3 to 3
- neighbors: int32 [8, 4, 27, 2048], P('gx', 'gy'), may hold values from 0 to 8384, as said below
- boundary: int32 [8, 4, 704], P('gx', 'gy'), may hold values from 0 to 2048, as said below
- counts: int32 [8, 4], P('gx', 'gy'), may hold values from 1 to 2048, as said below
Outputs:
- in_grad: bfloat16 [8, 4, 2048, 256], P('gx', 'gy')
- weight_grad: float32 [6912, 256], P(('gx', 'gy'))
- gamma_grad: float32 [256], replicated
- beta_grad: float32 [256], replicated
The draws below stay inside these ranges and needn't reach their ends.
Inputs may be any that keep to these rules, and one draw needn't show every extreme that they name: `neighbors`: the map is that of a submanifold convolution on a voxel grid: each device owns an 8 x 16 x 16 block of positions, its live rows are its occupied positions in order, rows at or past its count name no row at any offset, offset 13 names the row itself, and if pair (r, k) on one device names row q then row q's device names r at offset 26 - k. Rows named on other devices lie on that device's faces and are listed in its boundary list. `boundary`: A device's live rows on its x and y faces in increasing order, then 2048 in the unused slots. `counts`: some device holds 2048 live rows.
All inputs are finite; a program needn't handle non-finite values.
Results may differ from the reference program's by a relative error of at most 0.0049.
Values may be sent and summed in bfloat16 or wider, within the bound.
No kernel may reach another device: no remote copies, remote signals or barrier semaphores. Data moves between devices by JAX's collectives and lax.ppermute only.
A program may use at most 64 MiB of HBM per device.

```python
import jax
import jax.numpy as jnp
from jax import lax

C = 256
LX = 8
LY = 16
LZ = 16
R = 2048
HB = 704
SLABS = 8
STRIPS = 4


def geometry(key):
    base = jax.random.fold_in(key, 7)
    k_jit, k_full, k_roll = jax.random.split(base, 3)
    ndev = SLABS * STRIPS
    positions = LX * LY * LZ
    slab_ix = jnp.arange(SLABS, dtype=jnp.int32)[:, None]
    level = 250 + 750 * slab_ix * slab_ix // ((SLABS - 1) * (SLABS - 1))
    level = level + jax.random.randint(k_jit, (SLABS, STRIPS), -100, 101)
    level = jnp.clip(level, 150, 1000)
    full = jax.random.randint(k_full, (), 0, ndev)
    dev_ids = jnp.arange(ndev, dtype=jnp.int32).reshape(SLABS, STRIPS)
    level = jnp.where(dev_ids == full, 1000, level)
    rolled = jax.random.randint(k_roll, (SLABS, STRIPS, LX, LY, LZ), 0, 1000)
    active = (rolled < level[:, :, None, None, None]).astype(jnp.int32)
    flat = active.reshape(SLABS, STRIPS, positions)
    rowid = jnp.cumsum(flat, axis=2) - 1
    counts = jnp.sum(flat, axis=2).astype(jnp.int32)
    pos_x = jnp.arange(LX, dtype=jnp.int32)[:, None, None]
    pos_y = jnp.arange(LY, dtype=jnp.int32)[None, :, None]
    edge = (pos_x == 0) | (pos_x == LX - 1) | (pos_y == 0) | (pos_y == LY - 1)
    edge = jnp.broadcast_to(edge, (LX, LY, LZ)).reshape(positions).astype(jnp.int32)
    bflat = flat * edge[None, None, :]
    brank = jnp.cumsum(bflat, axis=2) - 1
    target = jnp.where(bflat == 1, brank, HB)

    def fill_one(where_to, rows_of):
        return jnp.full((HB + 1,), positions, jnp.int32).at[where_to].set(rows_of)[:HB]
    border = jax.vmap(jax.vmap(fill_one))(target, rowid)
    offs = jnp.arange(27, dtype=jnp.int32)
    off_x = (offs // 9 - 1)[None, None, :, None, None, None]
    off_y = (offs // 3 % 3 - 1)[None, None, :, None, None, None]
    off_z = (offs % 3 - 1)[None, None, :, None, None, None]
    big_i = jnp.arange(SLABS, dtype=jnp.int32)[:, None, None, None, None, None]
    big_j = jnp.arange(STRIPS, dtype=jnp.int32)[None, :, None, None, None, None]
    cell_x = jnp.arange(LX, dtype=jnp.int32)[None, None, None, :, None, None]
    cell_y = jnp.arange(LY, dtype=jnp.int32)[None, None, None, None, :, None]
    cell_z = jnp.arange(LZ, dtype=jnp.int32)[None, None, None, None, None, :]
    reach_x = big_i * LX + cell_x + off_x
    reach_y = big_j * LY + cell_y + off_y
    reach_z = cell_z + off_z
    inside = (reach_x >= 0) & (reach_x < SLABS * LX) & (reach_y >= 0) & (reach_y < STRIPS * LY) & (reach_z >= 0) & (reach_z < LZ)
    clip_x = jnp.clip(reach_x, 0, SLABS * LX - 1)
    clip_y = jnp.clip(reach_y, 0, STRIPS * LY - 1)
    clip_z = jnp.clip(reach_z, 0, LZ - 1)
    owner_i = clip_x // LX
    owner_j = clip_y // LY
    linear = (clip_x % LX * LY + clip_y % LY) * LZ + clip_z
    target_on = flat[owner_i, owner_j, linear]
    target_row = rowid[owner_i, owner_j, linear]
    target_rank = brank[owner_i, owner_j, linear]
    step_i = owner_i - big_i
    step_j = owner_j - big_j
    same = (step_i == 0) & (step_j == 0)
    index = jnp.where(same, target_row, positions + ((step_i + 1) * 3 + (step_j + 1)) * HB + target_rank)
    source_on = active[:, :, None, :, :, :]
    valid = inside & (target_on == 1) & (source_on == 1)
    index = jnp.where(valid, index, positions + 9 * HB).reshape(SLABS, STRIPS, 27, positions)
    dest = jnp.where(flat == 1, rowid, positions)

    def place(index_rows, dest_rows):
        return jnp.full((27, positions + 1), positions + 9 * HB, jnp.int32).at[:, dest_rows].set(index_rows)[:, :positions]
    mapped = jax.vmap(jax.vmap(place))(index, dest)
    return (mapped.astype(jnp.int32), border.astype(jnp.int32), counts)


def draw_neighbors(key, part):
    return geometry(key)[0]


def draw_boundary(key, part):
    return geometry(key)[1]


def draw_counts(key, part):
    return geometry(key)[2]


def draw_pre_norm(key, part):
    k_base, k_scale, k_mean = jax.random.split(jax.random.fold_in(key, 3), 3)
    ramp = (jnp.arange(SLABS, dtype=jnp.float32) / (SLABS - 1))[:, None, None, None]
    dev_scale = 1.0 + 2.0 * ramp
    chan_scale = jnp.exp(jax.random.uniform(k_scale, (C,), jnp.float32, 0.0, 2.3026))
    chan_mean = jax.random.normal(k_mean, (C,), jnp.float32) * 0.5
    noise = jax.random.normal(k_base, (SLABS, STRIPS, R, C), jnp.float32)
    return (noise * dev_scale * chan_scale + chan_mean * chan_scale + 0.5 * ramp).astype(jnp.bfloat16)


def strengthened(entries, own_key, source, target, shards_of, factor):
    owner, partner = [(jnp.arange(entries.shape[axis_at]) // (entries.shape[axis_at] // shards_of)).reshape([-1 if axis == axis_at else 1 for axis in range(entries.ndim)]) for axis_at in (source, target)]
    chosen = jax.random.permutation(own_key, shards_of)[partner]
    strong = (owner == chosen) | (owner == (partner + shards_of // 2) % shards_of)
    return jnp.where(strong, factor * entries, entries)


def level_of(own_key, extent, pieces, low, top_value):
    loudness, own = 1.0, jax.random.fold_in(own_key, 6)
    for position, parts in pieces:
        draws = jnp.exp(jax.random.uniform(jax.random.fold_in(own, position), (parts,), jnp.float32, low / len(pieces), top_value / len(pieces)))
        loudness = loudness * jnp.repeat(draws, extent[position] // parts).reshape([-1 if axis == position else 1 for axis in range(len(extent))])
    return loudness


def scatter_about(key, dims, width, limit, cuts=(), kind=jnp.bfloat16):
    result = width * jax.random.normal(key, dims, jnp.float32)
    if cuts:
        result = result * level_of(key, dims, cuts, -0.22, 0.18)
    return jnp.clip(result, -limit, limit).astype(kind)


def gaussian_with(rng, extent, deviation, most, pieces, heavy, kind=jnp.bfloat16):
    drawn = deviation * jax.random.normal(rng, extent, jnp.float32)
    if pieces:
        drawn = drawn * level_of(rng, extent, pieces, -0.22, 0.18)
    return jnp.clip(strengthened(drawn, jax.random.fold_in(rng, 3), *heavy), -most, most).astype(kind)


def setup_inputs(seed: int = 0) -> dict:
    splits = jax.random.split(jax.random.key(seed), 10)
    features = gaussian_with(splits[0], (SLABS, STRIPS, R, C), 1.0, 6.0, ((0, 8), (1, 4)), (0, 3, 8, 2.0))
    pre_norm = draw_pre_norm(jax.random.fold_in(splits[9], 71), 0)
    out_grad = scatter_about(splits[2], (SLABS, STRIPS, R, C), 1.0, 6.0, ((0, 8), (1, 4)))
    weight = scatter_about(splits[3], (27, C, C), C ** -0.5, 0.375)
    gamma = jnp.clip(1.0 + 0.18 * jax.random.normal(splits[4], (C,), jnp.float32), 0.1, 1.9)
    beta = scatter_about(splits[5], (C,), 0.5, 3.0, (), jnp.float32)
    neighbors = draw_neighbors(jax.random.fold_in(splits[9], 71), 0)
    boundary = draw_boundary(jax.random.fold_in(splits[9], 71), 0)
    counts = draw_counts(jax.random.fold_in(splits[9], 71), 0)
    return {"features": features, "pre_norm": pre_norm, "out_grad": out_grad, "weight": weight, "gamma": gamma, "beta": beta, "neighbors": neighbors, "boundary": boundary, "counts": counts}


def global_rows(neighbors, boundary):
    total = SLABS * STRIPS * R
    slab_ix = jnp.arange(SLABS, dtype=jnp.int32)[:, None, None, None]
    strip_ix = jnp.arange(STRIPS, dtype=jnp.int32)[None, :, None, None]
    local = neighbors < R
    absent = neighbors >= R + 9 * HB
    rel = jnp.clip(neighbors - R, 0, 9 * HB - 1)
    block = rel // HB
    slot = rel % HB
    near_x = jnp.clip(slab_ix + block // 3 - 1, 0, SLABS - 1)
    near_y = jnp.clip(strip_ix + block % 3 - 1, 0, STRIPS - 1)
    brow = boundary[near_x, near_y, slot]
    remote = jnp.where(brow >= R, total, (near_x * STRIPS + near_y) * R + brow)
    own = (slab_ix * STRIPS + strip_ix) * R + neighbors
    return jnp.where(local, own, jnp.where(absent, total, remote)).astype(jnp.int32)

def reference(features, pre_norm, out_grad, weight, gamma, beta, neighbors, boundary, counts):
    total = SLABS * STRIPS * R
    live = (jnp.arange(R, dtype=jnp.int32)[None, None, :] < counts[:, :, None])[..., None]
    zval = pre_norm.astype(jnp.float32)
    zlive = jnp.where(live, zval, jnp.float32(0.0))
    count = jnp.sum(counts).astype(jnp.float32)
    mean = lax.optimization_barrier(jnp.sum(zlive, axis=(0, 1, 2))) / count
    var = lax.optimization_barrier(jnp.sum(zlive * zval, axis=(0, 1, 2))) / count - mean * mean
    rstd = lax.rsqrt(var + 1e-05)
    zhat = (zval - mean) * rstd
    act = gamma * zhat + beta
    sig = jax.nn.sigmoid(act)
    grad_act = jnp.where(live, out_grad.astype(jnp.float32) * sig * (1.0 + act * (1.0 - sig)), jnp.float32(0.0))
    beta_grad = lax.optimization_barrier(jnp.sum(grad_act, axis=(0, 1, 2)))
    gamma_grad = lax.optimization_barrier(jnp.sum(grad_act * zhat, axis=(0, 1, 2)))
    dz = jnp.where(live, gamma * rstd * (grad_act - beta_grad / count - zhat * gamma_grad / count), jnp.float32(0.0)).astype(jnp.bfloat16)
    source = global_rows(neighbors, boundary)
    source_k = jnp.moveaxis(source, 2, 0).reshape(27, total)
    dz_flat = dz.reshape(total, C)
    x_padded = jnp.concatenate([features.reshape(total, C), jnp.zeros((1, C), jnp.bfloat16)], axis=0)

    def wgrad_one(index_row):
        picked = x_padded[index_row]
        return jnp.dot(picked.T, dz_flat, preferred_element_type=jnp.float32)
    weight_grad = lax.map(wgrad_one, source_k)

    def add_one(k, accum):
        contrib = jnp.dot(dz_flat, weight[k].T, preferred_element_type=jnp.float32)
        return accum.at[source_k[k]].add(contrib)
    accum = lax.fori_loop(0, 27, add_one, jnp.zeros((total + 1, C), jnp.float32))
    in_grad = accum[:total].reshape(SLABS, STRIPS, R, C).astype(jnp.bfloat16)
    return (in_grad, weight_grad.reshape(27 * C, C), gamma_grad, beta_grad)
```

```python
import functools

import jax
import jax.numpy as jnp
from jax import lax
from jax.experimental import pallas as pl
from jax.experimental.pallas import tpu as pltpu
from jax.sharding import PartitionSpec as P

TILE = 192
SEG = 16
LANES = 128
SEGS = 16
NOWHERE = -(1 << 20)
LISTED = 3
BF = jnp.bfloat16
F32 = jnp.float32
AXES = ("gx", "gy")


def everyone_sum(vec):
    count = lax.axis_size(AXES)
    spread = jnp.broadcast_to(vec[None], (count,) + vec.shape)
    return jnp.sum(lax.all_to_all(spread, AXES, 0, 0, tiled=True), axis=0)


def shift(block, axis):
    count = lax.axis_size(axis)
    forward = [(i, i + 1) for i in range(count - 1)]
    backward = [(target, source) for source, target in forward]
    return lax.ppermute(block, axis, forward), lax.ppermute(block, axis, backward)


def halve(arr, dim, axis, bit):
    count = lax.axis_size(axis)
    mine = (lax.axis_index(axis) >> bit) & 1
    give = lax.dynamic_index_in_dim(arr, 1 - mine, dim, keepdims=False).astype(BF)
    got = lax.ppermute(give, axis, [(i, i ^ (1 << bit)) for i in range(count)])
    keep = lax.dynamic_index_in_dim(arr, mine, dim, keepdims=False)
    return keep + got.astype(F32)


def scatter_sum(full):
    size_x, size_y = lax.axis_size("gx"), lax.axis_size("gy")
    rows, chans = full.shape
    bits_x, bits_y = size_x.bit_length() - 1, size_y.bit_length() - 1
    part = rows // (size_x * size_y)
    if (1 << bits_x) != size_x or (1 << bits_y) != size_y or bits_x < 1 or bits_y < 2:
        return lax.psum_scatter(full, AXES, scatter_dimension=0, tiled=True)
    arr = full.reshape((2,) * (bits_x + bits_y) + (part, chans))
    order = [("gx", b) for b in reversed(range(bits_x))] + [
        ("gy", b) for b in reversed(range(bits_y))
    ]

    def step(arr, order, which):
        dim = order.index(which)
        return halve(arr, dim, *which), order[:dim] + order[dim + 1 :]

    arr, order = step(arr, order, ("gy", 0))
    pair = [("gy", 1), ("gx", 0)]
    rest = [("gy", b) for b in range(2, bits_y)] + [("gx", b) for b in range(1, bits_x)]
    half = chans // 2
    colours = [(arr[..., :half], order), (arr[..., half:], order)]
    plans = [pair + rest, pair[::-1] + rest]
    for at in range(len(plans[0])):
        colours = [step(a, o, plan[at]) for (a, o), plan in zip(colours, plans)]
    return jnp.concatenate([a for a, _ in colours], axis=-1)


def plan_segments(links, rows, width, tiles):
    offsets = links.shape[0]
    total = rows + 9 * width
    groups = offsets // 3
    named = links < total
    clean = jnp.where(named, links, NOWHERE)
    clean = jnp.pad(clean, ((0, 0), (0, tiles * TILE - rows)), constant_values=NOWHERE)
    laid = clean.reshape(offsets, tiles, TILE).transpose(1, 0, 2)
    laid = jnp.pad(laid, ((0, 0), (0, -offsets % 8), (0, 0)), constant_values=NOWHERE)
    view = clean.reshape(groups, 3, tiles, TILE)
    low_ids, sizes = [], []
    for block in range(10):
        first = 0 if block == 0 else rows + (block - 1) * width
        last = rows if block == 0 else first + width
        inside = (view >= first) & (view < last)
        low = jnp.min(jnp.where(inside, view, total), axis=(1, 3)) // SEG
        high = jnp.max(jnp.where(inside, view, -1), axis=(1, 3))
        low_ids.append(low)
        sizes.append(jnp.where(high >= 0, high // SEG - low + 1, 0))
    low_ids = jnp.stack(low_ids, axis=-1).transpose(1, 0, 2).reshape(tiles * groups, 10)
    sizes = jnp.stack(sizes, axis=-1).transpose(1, 0, 2).reshape(tiles * groups, 10)
    ends = jnp.cumsum(sizes, axis=-1)
    starts = ends - sizes
    passes = (ends[:, -1] + SEGS - 1) // SEGS
    most = -(-(total // SEG) // SEGS)
    slot = lax.iota(jnp.int32, most * SEGS)[None, :, None]
    hit = (slot >= starts[:, None, :]) & (slot < ends[:, None, :])
    listed = jnp.sum(
        jnp.where(hit, low_ids[:, None, :] + slot - starts[:, None, :] + 1, 0), axis=-1
    ) - 1
    return laid, listed.reshape(tiles * groups, most, SEGS), passes


def conv_kernel(
    rows,
    width,
    seg_ref,
    pass_ref,
    all_segs,
    links_ref,
    dz_ref,
    mid_ref,
    low_ref,
    high_ref,
    feat_ref,
    w_ref,
    in_ref,
    wg_ref,
    table,
    cols,
    feat_t,
    acc,
    picked,
    spill,
    sems,
    spill_sem,
):
    tiles = links_ref.shape[0]
    offsets = w_ref.shape[0]
    groups = offsets // 3
    chans = feat_ref.shape[1]
    copies = [pltpu.make_async_copy(dz_ref, table.at[pl.ds(0, rows)], sems.at[0])]
    for da in range(3):
        for db, piece in enumerate((low_ref, mid_ref, high_ref)):
            copies.append(
                pltpu.make_async_copy(
                    piece.at[da],
                    table.at[pl.ds(rows + (3 * da + db) * width, width)],
                    sems.at[1 + 3 * da + db],
                )
            )
    for copy in copies:
        copy.start()

    def lay_tile(tile):
        slot = lax.rem(tile, 2)
        turned = jnp.transpose(links_ref[tile])
        for k in range(offsets):
            cols[slot, k] = jnp.broadcast_to(turned[:, k : k + 1], (TILE, LANES))
        start = pl.multiple_of(tile * TILE, TILE)
        feat_t[slot] = jnp.transpose(feat_ref[pl.ds(start, TILE), :])

    lane = lax.broadcasted_iota(jnp.int32, (1, LANES), 1)

    def gather(step, base_of):
        tile = step // groups
        group = lax.rem(step, groups)
        slot = lax.rem(tile, 2)
        bases = [base_of(j) for j in range(SEGS)]
        names = []
        for half in range(SEGS * SEG // LANES):
            per = LANES // SEG
            name = lane
            for j in range(per):
                off = bases[half * per + j] * SEG - j * SEG
                name = jnp.where(lane // SEG == j, lane + off, name)
            names.append(name)
        source = jnp.concatenate(
            [
                table[pl.ds(pl.multiple_of(jnp.maximum(b, 0) * SEG, SEG), SEG), :]
                for b in bases
            ],
            axis=0,
        )
        found = []
        for z in range(3):
            col = cols[slot, 3 * group + z]
            hot = [jnp.where(col == name, 1.0, 0.0).astype(BF) for name in names]
            found.append(
                jnp.dot(
                    jnp.concatenate(hot, axis=1), source, preferred_element_type=F32
                ).astype(BF)
            )
        return found

    def first_gather(step):
        found = gather(step, lambda j: seg_ref[step, j])
        buf = lax.rem(step, 2)
        for z in range(3):
            picked[buf, z] = found[z]

    def more_gather(step):
        count = pass_ref[step]

        @pl.when(count > 1)
        def _():
            @pl.loop(1, count)
            def _(p):
                @pl.when(p >= LISTED)
                def _():
                    copy = pltpu.make_async_copy(all_segs.at[step, p], spill, spill_sem)
                    copy.start()
                    copy.wait()

                @pl.when(p < LISTED)
                def _():
                    for j in range(SEGS):
                        spill[j] = seg_ref[step, p * SEGS + j]

                found = gather(step, lambda j: spill[j])
                buf = lax.rem(step, 2)
                for z in range(3):
                    picked[buf, z] += found[z]

    def products(step):
        tile = step // groups
        group = lax.rem(step, groups)
        slot = lax.rem(tile, 2)
        buf = lax.rem(step, 2)
        total = acc[...]
        for z in range(3):
            k = offsets - 1 - (3 * group + z)
            got = picked[buf, z]
            total = total + lax.dot_general(
                got, w_ref[k], (((1,), (1,)), ((), ())), preferred_element_type=F32
            )
            wg_ref[k] += jnp.dot(feat_t[slot], got, preferred_element_type=F32)
        acc[...] = total

    wg_ref[...] = jnp.zeros_like(wg_ref)
    acc[...] = jnp.zeros_like(acc)
    lay_tile(0)
    for copy in copies:
        copy.wait()
    first_gather(0)
    more_gather(0)
    steps = tiles * groups

    @pl.loop(0, steps)
    def _(step):
        tile = step // groups
        group = lax.rem(step, groups)
        following = jnp.minimum(step + 1, steps - 1)

        @pl.when((group == groups - 1) & (tile < tiles - 1))
        def _():
            lay_tile(tile + 1)

        first_gather(following)
        products(step)

        @pl.when(group == groups - 1)
        def _():
            start = pl.multiple_of(tile * TILE, TILE)
            left = rows - (tiles - 1) * TILE

            @pl.when(tile < tiles - 1)
            def _():
                in_ref[pl.ds(start, TILE), :] = acc[...].astype(BF)

            @pl.when(tile == tiles - 1)
            def _():
                in_ref[pl.ds((tiles - 1) * TILE, left), :] = acc[:left, :].astype(BF)

            acc[...] = jnp.zeros_like(acc)

        @pl.when(step + 1 < steps)
        def _():
            more_gather(following)


def convolve(plan, dz, mid, low, high, feat, weight):
    laid, listed, passes = plan
    rows, chans = dz.shape
    width = mid.shape[1]
    offsets = weight.shape[0]
    tiles = laid.shape[0]
    hbm = pl.BlockSpec(memory_space=pl.ANY)
    vmem = pl.BlockSpec(memory_space=pltpu.VMEM)
    smem = pl.BlockSpec(memory_space=pltpu.SMEM)
    listed_first = listed[:, :LISTED].reshape(listed.shape[0], LISTED * SEGS)
    feat = jnp.pad(feat, ((0, tiles * TILE - rows), (0, 0)))
    return pl.pallas_call(
        functools.partial(conv_kernel, rows, width),
        out_shape=(
            jax.ShapeDtypeStruct((rows, chans), BF),
            jax.ShapeDtypeStruct((offsets, chans, chans), F32),
        ),
        in_specs=[smem, smem, hbm, vmem, hbm, hbm, hbm, hbm, vmem, vmem],
        out_specs=(vmem, vmem),
        scratch_shapes=[
            pltpu.VMEM((rows + 9 * width, chans), BF),
            pltpu.VMEM((2, offsets, TILE, LANES), jnp.int32),
            pltpu.VMEM((2, chans, TILE), BF),
            pltpu.VMEM((TILE, chans), F32),
            pltpu.VMEM((2, 3, TILE, chans), BF),
            pltpu.SMEM((SEGS,), jnp.int32),
            pltpu.SemaphoreType.DMA((10,)),
            pltpu.SemaphoreType.DMA,
        ],
        compiler_params=pltpu.CompilerParams(vmem_limit_bytes=50 << 20),
        cost_estimate=pl.CostEstimate(
            flops=6 * offsets * rows * chans * chans,
            bytes_accessed=30 << 20,
            transcendentals=0,
        ),
    )(listed_first, passes, listed, laid, dz, mid, low, high, feat, weight)


def body(features, pre_norm, out_grad, weight, gamma, beta, neighbors, boundary, counts):
    feat = features[0, 0]
    rows, chans = feat.shape
    border = boundary[0, 0]
    links = neighbors[0, 0]
    width = border.shape[0]
    tiles = -(-rows // TILE)
    plan = plan_segments(links, rows, width, tiles)
    live = (lax.iota(jnp.int32, rows) < counts[0, 0])[:, None]
    zval = pre_norm[0, 0].astype(F32)
    zlive = jnp.where(live, zval, F32(0.0))
    own = jnp.stack(
        [
            jnp.sum(zlive, axis=0),
            jnp.sum(zlive * zval, axis=0),
            jnp.broadcast_to(counts[0, 0].astype(F32), (chans,)),
        ]
    )
    sums = everyone_sum(own)
    count = sums[2]
    mean = sums[0] / count
    var = sums[1] / count - mean * mean
    rstd = lax.rsqrt(var + 1e-05)
    zhat = (zval - mean) * rstd
    act = gamma * zhat + beta
    sig = jax.nn.sigmoid(act)
    grad_act = jnp.where(
        live, out_grad[0, 0].astype(F32) * sig * (1.0 + act * (1.0 - sig)), F32(0.0)
    )
    grads = everyone_sum(
        jnp.stack([jnp.sum(grad_act, axis=0), jnp.sum(grad_act * zhat, axis=0)])
    )
    beta_grad, gamma_grad = grads[0], grads[1]
    dz = jnp.where(
        live,
        gamma * rstd * (grad_act - beta_grad / count - zhat * gamma_grad / count),
        F32(0.0),
    ).astype(BF)
    edge = jnp.where(
        (border < rows)[:, None], jnp.take(dz, border, axis=0, mode="clip"), BF(0.0)
    )
    below, above = shift(edge, "gx")
    mid = jnp.stack([below, edge, above])
    low, high = shift(mid, "gy")
    in_grad, wgrad = convolve(plan, dz, mid, low, high, feat, weight)
    weight_grad = scatter_sum(wgrad.reshape(-1, chans))
    return (in_grad[None, None], weight_grad.reshape(-1, chans), gamma_grad, beta_grad)


def solution(mesh):
    placed = (
        P("gx", "gy", None, None),
        P("gx", "gy", None, None),
        P("gx", "gy", None, None),
        P(),
        P(),
        P(),
        P("gx", "gy", None, None),
        P("gx", "gy", None),
        P("gx", "gy"),
    )
    return jax.shard_map(
        body,
        mesh=mesh,
        in_specs=placed,
        out_specs=(P("gx", "gy", None, None), P(("gx", "gy"), None), P(), P()),
        check_vma=False,
    )
```

```python
import functools

import jax
import jax.numpy as jnp
from jax import lax
from jax.experimental import pallas as pl
from jax.experimental.pallas import tpu as pltpu
from jax.sharding import PartitionSpec as P


TILE = 192
SEG = 16
LANES = 128
SEGS = 16
LISTED = 2
NOWHERE = -(1 << 20)
BF = jnp.bfloat16
F32 = jnp.float32
AXES = ("gx", "gy")


def everyone_sum(vec):
    count = lax.axis_size(AXES)
    spread = jnp.broadcast_to(vec[None], (count,) + vec.shape)
    return jnp.sum(lax.all_to_all(spread, AXES, 0, 0, tiled=True), axis=0)


def shift(block, axis):
    count = lax.axis_size(axis)
    forward = [(i, i + 1) for i in range(count - 1)]
    backward = [(target, source) for source, target in forward]
    return lax.ppermute(block, axis, forward), lax.ppermute(block, axis, backward)


def halve(arr, dim, axis, bit):
    count = lax.axis_size(axis)
    mine = (lax.axis_index(axis) >> bit) & 1
    give = lax.dynamic_index_in_dim(arr, 1 - mine, dim, keepdims=False).astype(BF)
    got = lax.ppermute(give, axis, [(i, i ^ (1 << bit)) for i in range(count)])
    keep = lax.dynamic_index_in_dim(arr, mine, dim, keepdims=False)
    return keep + got.astype(F32)


def scatter_sum(full):
    size_x, size_y = lax.axis_size("gx"), lax.axis_size("gy")
    rows, chans = full.shape
    bits_x, bits_y = size_x.bit_length() - 1, size_y.bit_length() - 1
    part = rows // (size_x * size_y)
    if (1 << bits_x) != size_x or (1 << bits_y) != size_y or bits_x < 1 or bits_y < 2:
        return lax.psum_scatter(full, AXES, scatter_dimension=0, tiled=True)
    arr = full.reshape((2,) * (bits_x + bits_y) + (part, chans))
    order = [("gx", b) for b in reversed(range(bits_x))] + [
        ("gy", b) for b in reversed(range(bits_y))
    ]

    def step(arr, order, which):
        dim = order.index(which)
        return halve(arr, dim, *which), order[:dim] + order[dim + 1 :]

    arr, order = step(arr, order, ("gy", 0))
    pair = [("gy", 1), ("gx", 0)]
    rest = [("gy", b) for b in range(2, bits_y)] + [("gx", b) for b in range(1, bits_x)]
    half = chans // 2
    colours = [(arr[..., :half], order), (arr[..., half:], order)]
    plans = [pair + rest, pair[::-1] + rest]
    for at in range(len(plans[0])):
        colours = [step(a, o, plan[at]) for (a, o), plan in zip(colours, plans)]
    return jnp.concatenate([a for a, _ in colours], axis=-1)


def plan_segments(links, rows, width, tiles):
    offsets = links.shape[0]
    total = rows + 9 * width
    groups = offsets // 3
    clean = jnp.where(links < total, links, NOWHERE)
    clean = jnp.pad(clean, ((0, 0), (0, tiles * TILE - rows)), constant_values=NOWHERE)
    clean = clean.reshape(offsets, tiles, TILE)
    laid = jnp.pad(
        clean.transpose(1, 0, 2), ((0, 0), (0, -offsets % 8), (0, 0)), constant_values=NOWHERE
    )
    view = clean.reshape(groups, 3, tiles, TILE)
    lows, highs = [], []
    for stretch in range(10):
        first = 0 if stretch == 0 else rows + (stretch - 1) * width
        last = rows + stretch * width
        inside = (view >= first) & (view < last)
        lows.append(jnp.min(jnp.where(inside, view, total), axis=(1, 3)))
        highs.append(jnp.max(jnp.where(inside, view, -1), axis=(1, 3)))
    low, high = jnp.stack(lows) // SEG, jnp.stack(highs)
    sizes = jnp.where(high >= 0, high // SEG - low + 1, 0)
    order = lax.iota(jnp.int32, 10)
    upto = (order[None, :] <= order[:, None])[:, :, None, None]
    ends = jnp.sum(jnp.where(upto, sizes[None], 0), axis=1)
    starts = ends - sizes
    slot = lax.iota(jnp.int32, LISTED * SEGS).reshape(-1, 1, 1, 1)
    hit = (slot >= starts[None]) & (slot < ends[None])
    listed = jnp.sum(jnp.where(hit, low[None] + slot - starts[None] + 1, 0), axis=1) - 1
    return laid, listed, low, ends


def gather_kernel(rows, width, listed_ref, first_ref, end_ref, links_ref, *refs):
    (own_ref, *lines), (out_ref, table, spill, sems) = refs[:4], refs[4:]
    tile = pl.program_id(0)
    offsets = out_ref.shape[0]
    groups = offsets // 3

    @pl.when(tile == 0)
    def _():
        copies = [pltpu.make_async_copy(own_ref, table.at[pl.ds(0, rows)], sems.at[9])]
        for da in range(3):
            for db, line in enumerate((lines[1], lines[0], lines[2])):
                at = 3 * da + db
                place = table.at[pl.ds(rows + at * width, width)]
                copies.append(pltpu.make_async_copy(line.at[da], place, sems.at[at]))
        for copy in copies:
            copy.start()
        for copy in copies:
            copy.wait()

    lane = lax.broadcasted_iota(jnp.int32, (1, LANES), 1)
    turned = jnp.transpose(links_ref[0])

    def source_of(bases):
        names = []
        per = LANES // SEG
        for half in range(SEGS // per):
            name = lane
            for j in range(per):
                off = bases[half * per + j] * SEG - j * SEG
                name = jnp.where(lane // SEG == j, lane + off, name)
            names.append(name)
        source = jnp.concatenate(
            [
                table[pl.ds(pl.multiple_of(jnp.maximum(b, 0) * SEG, SEG), SEG), :]
                for b in bases
            ],
            axis=0,
        )
        return names, source

    def pick(col, names, source):
        hot = [jnp.where(col == name, 1.0, 0.0).astype(BF) for name in names]
        return jnp.dot(
            jnp.concatenate(hot, axis=1), source, preferred_element_type=F32
        ).astype(BF)

    most = jnp.int32(0)
    for group in range(groups):
        names, source = source_of([listed_ref[j, group, tile] for j in range(SEGS)])
        for z in range(3):
            k = 3 * group + z
            col = jnp.broadcast_to(turned[:, k : k + 1], (TILE, LANES))
            out_ref[offsets - 1 - k] = pick(col, names, source)
        most = jnp.maximum(most, end_ref[9, group, tile])

    @pl.when(most > SEGS)
    def _():
        @pl.loop(0, groups)
        def _(group):
            count = (end_ref[9, group, tile] + SEGS - 1) // SEGS

            @pl.loop(1, count)
            def _(p):
                @pl.when(p < LISTED)
                def _():
                    for j in range(SEGS):
                        spill[j] = listed_ref[p * SEGS + j, group, tile]

                @pl.when(p >= LISTED)
                def _():
                    @pl.loop(0, SEGS)
                    def _(j):
                        slot = p * SEGS + j
                        base = jnp.int32(-1)
                        start = jnp.int32(0)
                        for block in range(10):
                            end = end_ref[block, group, tile]
                            here = (slot >= start) & (slot < end)
                            first = first_ref[block, group, tile]
                            base = jnp.where(here, first + slot - start, base)
                            start = end
                        spill[j] = base

                names, source = source_of([spill[j] for j in range(SEGS)])
                which = lax.broadcasted_iota(jnp.int32, turned.shape, 1)
                for z in range(3):
                    k = 3 * group + z
                    col = jnp.sum(
                        jnp.where(which == k, turned, 0), axis=1, keepdims=True
                    )
                    more = pick(jnp.broadcast_to(col, (TILE, LANES)), names, source)
                    out_ref[offsets - 1 - k] += more


def gather_all(plan, offsets, pieces):
    laid, listed, low, ends = plan
    rows, chans = pieces[0].shape
    width = pieces[1].shape[1]
    tiles = laid.shape[0]
    smem = pl.BlockSpec(memory_space=pltpu.SMEM)
    return pl.pallas_call(
        functools.partial(gather_kernel, rows, width),
        grid=(tiles,),
        out_shape=jax.ShapeDtypeStruct((offsets, rows, chans), BF),
        in_specs=[smem, smem, smem]
        + [pl.BlockSpec((1,) + laid.shape[1:], lambda i: (i, 0, 0))]
        + [pl.BlockSpec(memory_space=pl.ANY)] * 4,
        out_specs=pl.BlockSpec((offsets, TILE, chans), lambda i: (0, i, 0)),
        scratch_shapes=[
            pltpu.VMEM((rows + 9 * width, chans), BF),
            pltpu.SMEM((SEGS,), jnp.int32),
            pltpu.SemaphoreType.DMA((10,)),
        ],
        compiler_params=pltpu.CompilerParams(vmem_limit_bytes=56 << 20),
        cost_estimate=pl.CostEstimate(
            flops=2 * offsets * rows * chans * SEGS * SEG,
            bytes_accessed=2 * offsets * rows * chans,
            transcendentals=0,
        ),
    )(listed, low, ends, laid, *pieces)


def outer_kernel(turned_ref, got_ref, out_ref):
    chans = turned_ref.shape[0]
    for k in range(got_ref.shape[0]):
        out_ref[k * chans : (k + 1) * chans] = jnp.dot(
            turned_ref[...], got_ref[k], preferred_element_type=F32
        )


def outer_products(turned, got):
    chans, rows = turned.shape
    offsets = got.shape[0]
    return pl.pallas_call(
        outer_kernel,
        grid=(offsets // 3,),
        out_shape=jax.ShapeDtypeStruct((offsets * chans, chans), F32),
        in_specs=[
            pl.BlockSpec((chans, rows), lambda k: (0, 0)),
            pl.BlockSpec((3, rows, chans), lambda k: (k, 0, 0)),
        ],
        out_specs=pl.BlockSpec((3 * chans, chans), lambda k: (k, 0)),
        compiler_params=pltpu.CompilerParams(vmem_limit_bytes=56 << 20),
        cost_estimate=pl.CostEstimate(
            flops=2 * offsets * rows * chans * chans,
            bytes_accessed=2 * offsets * rows * chans,
            transcendentals=0,
        ),
    )(turned, got)


def back_kernel(got_ref, w_ref, out_ref):
    offsets = w_ref.shape[0]
    total = lax.dot_general(
        jnp.concatenate([got_ref[k] for k in range(offsets)], axis=1),
        jnp.concatenate([w_ref[k] for k in range(offsets)], axis=1),
        (((1,), (1,)), ((), ())),
        preferred_element_type=F32,
    )
    out_ref[...] = total.astype(BF)


def back_products(got, weight, first, last):
    offsets, chans, _ = weight.shape
    count = last - first
    block = 256 if count % 256 == 0 else count
    return pl.pallas_call(
        back_kernel,
        grid=(count // block,),
        out_shape=jax.ShapeDtypeStruct((count, chans), BF),
        in_specs=[
            pl.BlockSpec((offsets, block, chans), lambda i: (0, i + first // block, 0)),
            pl.BlockSpec(weight.shape, lambda i: (0, 0, 0)),
        ],
        out_specs=pl.BlockSpec((block, chans), lambda i: (i, 0)),
        compiler_params=pltpu.CompilerParams(vmem_limit_bytes=56 << 20),
        cost_estimate=pl.CostEstimate(
            flops=2 * offsets * count * chans * chans,
            bytes_accessed=2 * offsets * count * chans,
            transcendentals=0,
        ),
    )(got, weight)


def table_pieces(own, border):
    edge = jnp.take(own, border, axis=0, mode="clip")
    below, above = shift(edge, "gx")
    line = jnp.stack([below, edge, above])
    low, high = shift(line, "gy")
    return own, line, low, high


def step(features, pre_norm, out_grad, weight, gamma, beta, neighbors, boundary, counts):
    feat = features[0, 0]
    rows, chans = feat.shape
    border = boundary[0, 0]
    links = neighbors[0, 0]
    offsets = links.shape[0]
    width = border.shape[0]
    tiles = -(-rows // TILE)
    plan = plan_segments(links, rows, width, tiles)
    turned = feat.T
    live = (lax.iota(jnp.int32, rows) < counts[0, 0])[:, None]
    zval = pre_norm[0, 0].astype(F32)
    zlive = jnp.where(live, zval, F32(0.0))
    own = jnp.stack(
        [
            jnp.sum(zlive, axis=0),
            jnp.sum(zlive * zval, axis=0),
            jnp.broadcast_to(counts[0, 0].astype(F32), (chans,)),
        ]
    )
    sums = everyone_sum(own)
    count = sums[2]
    mean = sums[0] / count
    var = sums[1] / count - mean * mean
    rstd = lax.rsqrt(var + 1e-05)
    zhat = (zval - mean) * rstd
    act = gamma * zhat + beta
    sig = jax.nn.sigmoid(act)
    grad_act = jnp.where(
        live, out_grad[0, 0].astype(F32) * sig * (1.0 + act * (1.0 - sig)), F32(0.0)
    )
    pair = jnp.stack([jnp.sum(grad_act, axis=0), jnp.sum(grad_act * zhat, axis=0)])
    grads = everyone_sum(pair)
    beta_grad, gamma_grad = grads[0], grads[1]
    dz = jnp.where(
        live,
        gamma * rstd * (grad_act - beta_grad / count - zhat * gamma_grad / count),
        F32(0.0),
    ).astype(BF)
    pieces = table_pieces(dz, border)
    near = gather_all(plan, offsets, pieces)
    wgrad = outer_products(turned, near)
    weight_grad = scatter_sum(wgrad)
    cut = rows // 8 * 5
    in_grad = [back_products(near, weight, 0, cut)]
    in_grad.append(back_products(near, weight, cut, rows))
    in_grad = jnp.concatenate(in_grad)
    return (in_grad[None, None], weight_grad.reshape(-1, chans), gamma_grad, beta_grad)


def solution(mesh):
    placed = (
        P("gx", "gy", None, None),
        P("gx", "gy", None, None),
        P("gx", "gy", None, None),
        P(),
        P(),
        P(),
        P("gx", "gy", None, None),
        P("gx", "gy", None),
        P("gx", "gy"),
    )
    return jax.shard_map(
        step,
        mesh=mesh,
        in_specs=placed,
        out_specs=(P("gx", "gy", None, None), P(("gx", "gy"), None), P(), P()),
        check_vma=False,
    )
```

```python
import functools

import jax
import jax.numpy as jnp
from jax import lax
from jax.experimental import pallas as pl
from jax.experimental.pallas import tpu as pltpu
from jax.sharding import PartitionSpec as P


TILE = 176
SEG = 16
LANES = 128
SEGS = 16
LISTED = 2
NOWHERE = -(1 << 20)
BF = jnp.bfloat16
F32 = jnp.float32
AXES = ("gx", "gy")


def from_everyone(vec):
    count = lax.axis_size(AXES)
    spread = jnp.broadcast_to(vec[None], (count,) + vec.shape)
    return lax.all_to_all(spread, AXES, 0, 0, tiled=True)


def shift(up, down, axis):
    count = lax.axis_size(axis)
    forward = [(i, i + 1) for i in range(count - 1)]
    backward = [(target, source) for source, target in forward]
    return lax.ppermute(up, axis, forward), lax.ppermute(down, axis, backward)


def halve(arr, dim, axis, bit):
    count = lax.axis_size(axis)
    mine = (lax.axis_index(axis) >> bit) & 1
    give = lax.dynamic_index_in_dim(arr, 1 - mine, dim, keepdims=False).astype(BF)
    got = lax.ppermute(give, axis, [(i, i ^ (1 << bit)) for i in range(count)])
    keep = lax.dynamic_index_in_dim(arr, mine, dim, keepdims=False)
    return keep + got.astype(F32)


def scatter_sum(full):
    size_x, size_y = lax.axis_size("gx"), lax.axis_size("gy")
    rows, chans = full.shape
    bits_x, bits_y = size_x.bit_length() - 1, size_y.bit_length() - 1
    part = rows // (size_x * size_y)
    if (1 << bits_x) != size_x or (1 << bits_y) != size_y or bits_x < 1 or bits_y < 2:
        return lax.psum_scatter(full, AXES, scatter_dimension=0, tiled=True)
    arr = full.reshape((2,) * (bits_x + bits_y) + (part, chans))
    order = [("gx", b) for b in reversed(range(bits_x))] + [
        ("gy", b) for b in reversed(range(bits_y))
    ]

    def step(arr, order, which):
        dim = order.index(which)
        return halve(arr, dim, *which), order[:dim] + order[dim + 1 :]

    arr, order = step(arr, order, ("gy", 0))
    pair = [("gy", 1), ("gx", 0)]
    rest = [("gy", b) for b in range(2, bits_y)] + [("gx", b) for b in range(1, bits_x)]
    half = chans // 2
    colours = [(arr[..., :half], order), (arr[..., half:], order)]
    plans = [pair + rest, pair[::-1] + rest]
    for at in range(len(plans[0])):
        colours = [step(a, o, plan[at]) for (a, o), plan in zip(colours, plans)]
    return jnp.concatenate([a for a, _ in colours], axis=-1)


def plan_segments(links, rows, width, tiles):
    offsets = links.shape[0]
    total = rows + 9 * width
    groups = offsets // 3
    clean = jnp.where(links < total, links, NOWHERE)
    clean = jnp.pad(clean, ((0, 0), (0, tiles * TILE - rows)), constant_values=NOWHERE)
    laid = clean.reshape(groups, 3, tiles * TILE)
    laid = jnp.pad(laid, ((0, 0), (0, 5), (0, 0)), constant_values=NOWHERE)
    view = clean.reshape(groups, 3, tiles, TILE)
    lows, highs = [], []
    for stretch in range(10):
        first = 0 if stretch == 0 else rows + (stretch - 1) * width
        last = rows + stretch * width
        inside = (view >= first) & (view < last)
        lows.append(jnp.min(jnp.where(inside, view, total), axis=(1, 3)))
        highs.append(jnp.max(jnp.where(inside, view, -1), axis=(1, 3)))
    low, high = jnp.stack(lows) // SEG, jnp.stack(highs)
    sizes = jnp.where(high >= 0, high // SEG - low + 1, 0)
    order = lax.iota(jnp.int32, 10)
    upto = (order[None, :] <= order[:, None])[:, :, None, None]
    ends = jnp.sum(jnp.where(upto, sizes[None], 0), axis=1)
    starts = ends - sizes
    slot = lax.iota(jnp.int32, LISTED * SEGS).reshape(-1, 1, 1, 1)
    hit = (slot >= starts[None]) & (slot < ends[None])
    listed = jnp.sum(jnp.where(hit, low[None] + slot - starts[None] + 1, 0), axis=1) - 1
    return laid, listed, low, ends


def gather_kernel(
    rows,
    width,
    listed_ref,
    first_ref,
    end_ref,
    begin_ref,
    links_ref,
    own_ref,
    edge_ref,
    low_ref,
    high_ref,
    pair_ref,
    low_pair_ref,
    high_pair_ref,
    turned_ref,
    feat_ref,
    got_ref,
    wg_ref,
    table,
    columns,
    spill,
    sems,
):
    group = pl.program_id(0)
    chans = table.shape[1]
    tiles = links_ref.shape[2] // TILE

    @pl.when(group == 0)
    def _():
        copies = [pltpu.make_async_copy(own_ref, table.at[pl.ds(0, rows)], sems.at[9])]
        for db, side in enumerate((low_ref, edge_ref, high_ref)):
            place = table.at[pl.ds(rows + (3 + db) * width, width)]
            copies.append(pltpu.make_async_copy(side, place, sems.at[3 + db]))
        part = pair_ref.shape[1]
        for da in range(2):
            for db, pair in enumerate((low_pair_ref, pair_ref, high_pair_ref)):
                at = 6 * da + db
                start = pl.multiple_of(rows + at * width + begin_ref[at], SEG)
                place = table.at[pl.ds(start, part)]
                copies.append(pltpu.make_async_copy(pair.at[da], place, sems.at[at]))
        for copy in copies:
            copy.start()
        for copy in copies:
            copy.wait()

    lane = lax.broadcasted_iota(jnp.int32, (1, LANES), 1)

    def source_of(bases):
        names = []
        per = LANES // SEG
        for half in range(SEGS // per):
            name = lane
            for j in range(per):
                off = bases[half * per + j] * SEG - j * SEG
                name = jnp.where(lane // SEG == j, lane + off, name)
            names.append(name)
        source = jnp.concatenate(
            [
                table[pl.ds(pl.multiple_of(jnp.maximum(b, 0) * SEG, SEG), SEG), :]
                for b in bases
            ],
            axis=0,
        )
        return names, source

    def pick(col, names, source):
        wide = jnp.broadcast_to(col, (col.shape[0], LANES))
        hot = [jnp.where(wide == name, 1.0, 0.0).astype(BF) for name in names]
        return jnp.dot(
            jnp.concatenate(hot, axis=1), source, preferred_element_type=F32
        ).astype(BF)

    upright = jnp.transpose(links_ref[0])
    most = jnp.int32(0)
    for tile in range(tiles):
        start, stop = tile * TILE, min((tile + 1) * TILE, rows)
        names, source = source_of([listed_ref[j, group, tile] for j in range(SEGS)])
        for z in range(3):
            got_ref[2 - z, start:stop] = pick(upright[start:stop, z : z + 1], names, source)
        most = jnp.maximum(most, end_ref[9, group, tile])
    for z in range(3):
        wg_ref[z * chans : (z + 1) * chans] = jnp.dot(
            turned_ref[...], got_ref[z], preferred_element_type=F32
        )

    @pl.when(most > SEGS)
    def _():
        columns[...] = upright

        @pl.loop(0, tiles)
        def _(tile):
            count = (end_ref[9, group, tile] + SEGS - 1) // SEGS
            start = pl.multiple_of(jnp.minimum(tile * TILE, rows - TILE), SEG)
            row = start + lax.broadcasted_iota(jnp.int32, (TILE, 1), 0)
            fresh = row >= tile * TILE

            @pl.loop(1, count)
            def _(p):
                @pl.when(p < LISTED)
                def _():
                    for j in range(SEGS):
                        spill[j] = listed_ref[p * SEGS + j, group, tile]

                @pl.when(p >= LISTED)
                def _():
                    @pl.loop(0, SEGS)
                    def _(j):
                        slot = p * SEGS + j
                        base = jnp.int32(-1)
                        begin = jnp.int32(0)
                        for block in range(10):
                            end = end_ref[block, group, tile]
                            here = (slot >= begin) & (slot < end)
                            first = first_ref[block, group, tile]
                            base = jnp.where(here, first + slot - begin, base)
                            begin = end
                        spill[j] = base

                names, source = source_of([spill[j] for j in range(SEGS)])
                beside = feat_ref[pl.ds(start, TILE), :]
                for z in range(3):
                    col = columns[pl.ds(start, TILE), z : z + 1]
                    more = pick(jnp.where(fresh, col, NOWHERE), names, source)
                    got_ref[2 - z, pl.ds(start, TILE)] += more
                    wg_ref[(2 - z) * chans : (3 - z) * chans] += lax.dot_general(
                        beside, more, (((0,), (0,)), ((), ())), preferred_element_type=F32
                    )


def gather_outer(plan, pieces, feat, turned):
    laid, listed, low, ends = plan
    rows, chans = feat.shape
    begins, *pieces = pieces
    width = pieces[1].shape[0]
    groups = laid.shape[0]
    smem = pl.BlockSpec(memory_space=pltpu.SMEM)
    return pl.pallas_call(
        functools.partial(gather_kernel, rows, width),
        grid=(groups,),
        out_shape=(
            jax.ShapeDtypeStruct((3 * groups, rows, chans), BF),
            jax.ShapeDtypeStruct((3 * groups * chans, chans), F32),
        ),
        in_specs=[smem] * 4
        + [pl.BlockSpec((1,) + laid.shape[1:], lambda g: (g, 0, 0))]
        + [pl.BlockSpec(memory_space=pl.ANY)] * 7
        + [
            pl.BlockSpec((chans, rows), lambda g: (0, 0)),
            pl.BlockSpec((rows, chans), lambda g: (0, 0)),
        ],
        out_specs=(
            pl.BlockSpec((3, rows, chans), lambda g: (groups - 1 - g, 0, 0)),
            pl.BlockSpec((3 * chans, chans), lambda g: (groups - 1 - g, 0)),
        ),
        scratch_shapes=[
            pltpu.VMEM((rows + 9 * width, chans), BF),
            pltpu.VMEM((laid.shape[2], laid.shape[1]), jnp.int32),
            pltpu.SMEM((SEGS,), jnp.int32),
            pltpu.SemaphoreType.DMA((10,)),
        ],
        compiler_params=pltpu.CompilerParams(vmem_limit_bytes=56 << 20),
        cost_estimate=pl.CostEstimate(
            flops=12 * groups * rows * chans * chans,
            bytes_accessed=6 * groups * rows * chans,
            transcendentals=0,
        ),
    )(listed, low, ends, begins, laid, *pieces, turned, feat)


def back_kernel(got_ref, w_ref, out_ref):
    offsets = w_ref.shape[0]
    total = lax.dot_general(
        jnp.concatenate([got_ref[k] for k in range(offsets)], axis=1),
        jnp.concatenate([w_ref[k] for k in range(offsets)], axis=1),
        (((1,), (1,)), ((), ())),
        preferred_element_type=F32,
    )
    out_ref[...] = total.astype(BF)


def back_products(got, weight, first, last):
    offsets, chans, _ = weight.shape
    count = last - first
    block = 256 if count % 256 == 0 else count
    return pl.pallas_call(
        back_kernel,
        grid=(count // block,),
        out_shape=jax.ShapeDtypeStruct((count, chans), BF),
        in_specs=[
            pl.BlockSpec((offsets, block, chans), lambda i: (0, i + first // block, 0)),
            pl.BlockSpec(weight.shape, lambda i: (0, 0, 0)),
        ],
        out_specs=pl.BlockSpec((block, chans), lambda i: (i, 0)),
        compiler_params=pltpu.CompilerParams(vmem_limit_bytes=56 << 20),
        cost_estimate=pl.CostEstimate(
            flops=2 * offsets * count * chans * chans,
            bytes_accessed=2 * offsets * count * chans,
            transcendentals=0,
        ),
    )(got, weight)


def window_of(used, width):
    part = -(-(width // 2) // SEG) * SEG
    return part, -(-jnp.maximum(used - part, 0) // SEG) * SEG


def table_pieces(own, border, used_by):
    rows, width = own.shape[0], border.shape[0]
    size_x, size_y = lax.axis_size("gx"), lax.axis_size("gy")
    at_x, at_y = lax.axis_index("gx"), lax.axis_index("gy")
    part, start = window_of(jnp.sum((border < rows).astype(jnp.int32)), width)
    below = (at_x - 1) * size_y + at_y + jnp.arange(-1, 2)
    below = jnp.clip(below, 0, size_x * size_y - 1)
    _, begins = window_of(used_by[below], width)
    begins = jnp.concatenate([begins, jnp.zeros((6,), jnp.int32)])
    edge = jnp.take(own, border, axis=0, mode="clip")
    upper = lax.dynamic_slice_in_dim(edge, start, part, axis=0)
    pair = jnp.stack(shift(upper, edge[:part], "gx"))
    low, high = shift(edge, edge, "gy")
    low_pair, high_pair = shift(pair, pair, "gy")
    return begins, own, edge, low, high, pair, low_pair, high_pair


def step(features, pre_norm, out_grad, weight, gamma, beta, neighbors, boundary, counts):
    feat = features[0, 0]
    rows, chans = feat.shape
    border = boundary[0, 0]
    links = neighbors[0, 0]
    width = border.shape[0]
    tiles = -(-rows // TILE)
    plan = plan_segments(links, rows, width, tiles)
    turned = feat.T
    live = (lax.iota(jnp.int32, rows) < counts[0, 0])[:, None]
    zval = pre_norm[0, 0].astype(F32)
    zlive = jnp.where(live, zval, F32(0.0))
    own = jnp.stack(
        [
            jnp.sum(zlive, axis=0),
            jnp.sum(zlive * zval, axis=0),
            jnp.broadcast_to(counts[0, 0].astype(F32), (chans,)),
            jnp.broadcast_to(jnp.sum((border < rows).astype(F32)), (chans,)),
        ]
    )
    every = from_everyone(own)
    sums = jnp.sum(every, axis=0)
    count = sums[2]
    mean = sums[0] / count
    var = sums[1] / count - mean * mean
    rstd = lax.rsqrt(var + 1e-05)
    zhat = (zval - mean) * rstd
    act = gamma * zhat + beta
    sig = jax.nn.sigmoid(act)
    grad_act = jnp.where(
        live, out_grad[0, 0].astype(F32) * sig * (1.0 + act * (1.0 - sig)), F32(0.0)
    )
    pair = jnp.stack([jnp.sum(grad_act, axis=0), jnp.sum(grad_act * zhat, axis=0)])
    grads = jnp.sum(from_everyone(pair), axis=0)
    beta_grad, gamma_grad = grads[0], grads[1]
    dz = jnp.where(
        live,
        gamma * rstd * (grad_act - beta_grad / count - zhat * gamma_grad / count),
        F32(0.0),
    ).astype(BF)
    pieces = table_pieces(dz, border, every[:, 3, 0].astype(jnp.int32))
    near, wgrad = gather_outer(plan, pieces, feat, turned)
    weight_grad = scatter_sum(wgrad)
    cut = rows // 8 * 5
    in_grad = [back_products(near, weight, 0, cut)]
    in_grad.append(back_products(near, weight, cut, rows))
    in_grad = jnp.concatenate(in_grad)
    return (in_grad[None, None], weight_grad.reshape(-1, chans), gamma_grad, beta_grad)


def solution(mesh):
    placed = (
        P("gx", "gy", None, None),
        P("gx", "gy", None, None),
        P("gx", "gy", None, None),
        P(),
        P(),
        P(),
        P("gx", "gy", None, None),
        P("gx", "gy", None),
        P("gx", "gy"),
    )
    return jax.shard_map(
        step,
        mesh=mesh,
        in_specs=placed,
        out_specs=(P("gx", "gy", None, None), P(("gx", "gy"), None), P(), P()),
        check_vma=False,
    )
```

```python
import functools

import jax
import jax.numpy as jnp
from jax import lax
from jax.experimental import pallas as pl
from jax.experimental.pallas import tpu as pltpu
from jax.sharding import PartitionSpec as P


TILE = 176
SEG = 16
LANES = 128
SEGS = 16
PARTS = 9
LISTED = 2
NOWHERE = -(1 << 20)
BF = jnp.bfloat16
F32 = jnp.float32
AXES = ("gx", "gy")


def from_everyone(vec):
    count = lax.axis_size(AXES)
    spread = jnp.broadcast_to(vec[None], (count,) + vec.shape)
    return lax.all_to_all(spread, AXES, 0, 0, tiled=True)


def shift(up, down, axis):
    count = lax.axis_size(axis)
    forward = [(i, i + 1) for i in range(count - 1)]
    backward = [(target, source) for source, target in forward]
    return lax.ppermute(up, axis, forward), lax.ppermute(down, axis, backward)


def halve(arr, dim, axis, bit):
    count = lax.axis_size(axis)
    mine = (lax.axis_index(axis) >> bit) & 1
    give = lax.dynamic_index_in_dim(arr, 1 - mine, dim, keepdims=False).astype(BF)
    got = lax.ppermute(give, axis, [(i, i ^ (1 << bit)) for i in range(count)])
    keep = lax.dynamic_index_in_dim(arr, mine, dim, keepdims=False)
    return keep + got.astype(F32)


def scatter_sum(full):
    size_x, size_y = lax.axis_size("gx"), lax.axis_size("gy")
    rows, chans = full.shape
    bits_x, bits_y = size_x.bit_length() - 1, size_y.bit_length() - 1
    part = rows // (size_x * size_y)
    if (1 << bits_x) != size_x or (1 << bits_y) != size_y or bits_x < 1 or bits_y < 2:
        return lax.psum_scatter(full, AXES, scatter_dimension=0, tiled=True)
    arr = full.reshape((2,) * (bits_x + bits_y) + (part, chans))
    order = [("gx", b) for b in reversed(range(bits_x))] + [
        ("gy", b) for b in reversed(range(bits_y))
    ]

    def step(arr, order, which):
        dim = order.index(which)
        return halve(arr, dim, *which), order[:dim] + order[dim + 1 :]

    arr, order = step(arr, order, ("gy", 0))
    pair = [("gy", 1), ("gx", 0)]
    rest = [("gy", b) for b in range(2, bits_y)] + [("gx", b) for b in range(1, bits_x)]
    half = chans // 2
    colours = [(arr[..., :half], order), (arr[..., half:], order)]
    plans = [pair + rest, pair[::-1] + rest]
    for at in range(len(plans[0])):
        colours = [step(a, o, plan[at]) for (a, o), plan in zip(colours, plans)]
    return jnp.concatenate([a for a, _ in colours], axis=-1)


def plan_segments(links, rows, width, tiles):
    offsets = links.shape[0]
    total = rows + 9 * width
    groups = offsets // 3
    clean = jnp.where(links < total, links, NOWHERE)
    clean = jnp.pad(clean, ((0, 0), (0, tiles * TILE - rows)), constant_values=NOWHERE)
    laid = clean.reshape(groups, 3, tiles * TILE)
    laid = jnp.pad(laid, ((0, 0), (0, 5), (0, 0)), constant_values=NOWHERE)
    view = clean.reshape(groups, 3, tiles, TILE)
    lows, highs = [], []
    for stretch in range(10):
        first = 0 if stretch == 0 else rows + (stretch - 1) * width
        last = rows + stretch * width
        inside = (view >= first) & (view < last)
        lows.append(jnp.min(jnp.where(inside, view, total), axis=(1, 3)))
        highs.append(jnp.max(jnp.where(inside, view, -1), axis=(1, 3)))
    low, high = jnp.stack(lows) // SEG, jnp.stack(highs)
    sizes = jnp.where(high >= 0, high // SEG - low + 1, 0)
    order = lax.iota(jnp.int32, 10)
    upto = (order[None, :] <= order[:, None])[:, :, None, None]
    ends = jnp.sum(jnp.where(upto, sizes[None], 0), axis=1)
    starts = ends - sizes
    slot = lax.iota(jnp.int32, LISTED * SEGS).reshape(-1, 1, 1, 1)
    hit = (slot >= starts[None]) & (slot < ends[None])
    listed = jnp.sum(jnp.where(hit, low[None] + slot - starts[None] + 1, 0), axis=1) - 1
    return laid, listed, low, ends


def gather_kernel(
    rows,
    width,
    listed_ref,
    first_ref,
    end_ref,
    begin_ref,
    links_ref,
    own_ref,
    edge_ref,
    low_ref,
    high_ref,
    pair_ref,
    low_pair_ref,
    high_pair_ref,
    turned_ref,
    feat_ref,
    got_ref,
    wg_ref,
    table,
    columns,
    spill,
    sems,
):
    group = pl.program_id(0)
    chans = table.shape[1]
    tiles = links_ref.shape[2] // TILE

    @pl.when(group == 0)
    def _():
        copies = [pltpu.make_async_copy(own_ref, table.at[pl.ds(0, rows)], sems.at[9])]
        for db, side in enumerate((low_ref, edge_ref, high_ref)):
            place = table.at[pl.ds(rows + (3 + db) * width, width)]
            copies.append(pltpu.make_async_copy(side, place, sems.at[3 + db]))
        part = pair_ref.shape[1]
        for da in range(2):
            for db, pair in enumerate((low_pair_ref, pair_ref, high_pair_ref)):
                at = 6 * da + db
                start = pl.multiple_of(rows + at * width + begin_ref[at], SEG)
                place = table.at[pl.ds(start, part)]
                copies.append(pltpu.make_async_copy(pair.at[da], place, sems.at[at]))
        for copy in copies:
            copy.start()
        for copy in copies:
            copy.wait()

    lane = lax.broadcasted_iota(jnp.int32, (1, LANES), 1)

    def source_of(bases):
        names = []
        per = LANES // SEG
        for half in range(SEGS // per):
            name = lane
            for j in range(per):
                off = bases[half * per + j] * SEG - j * SEG
                name = jnp.where(lane // SEG == j, lane + off, name)
            names.append(name)
        source = jnp.concatenate(
            [
                table[pl.ds(pl.multiple_of(jnp.maximum(b, 0) * SEG, SEG), SEG), :]
                for b in bases
            ],
            axis=0,
        )
        return names, source

    def pick(col, names, source):
        wide = jnp.broadcast_to(col, (col.shape[0], LANES))
        hot = [jnp.where(wide == name, 1.0, 0.0).astype(BF) for name in names]
        return jnp.dot(
            jnp.concatenate(hot, axis=1), source, preferred_element_type=F32
        ).astype(BF)

    groups = links_ref.shape[0]
    slot = lax.rem(group, 2)

    @pl.when(group == 0)
    def _():
        columns[0] = jnp.transpose(links_ref[0])

    most = jnp.int32(0)
    for tile in range(tiles):
        most = jnp.maximum(most, end_ref[9, group, tile])
    for z in range(3):
        for tile in range(tiles):
            start, stop = tile * TILE, min((tile + 1) * TILE, rows)
            names, source = source_of([listed_ref[j, group, tile] for j in range(SEGS)])
            col = columns[slot, start:stop, z : z + 1]
            got_ref[2 - z, start:stop] = pick(col, names, source)
        if z == 2:
            columns[1 - slot] = jnp.transpose(links_ref[jnp.minimum(group + 1, groups - 1)])
        wg_ref[(2 - z) * chans : (3 - z) * chans] = jnp.dot(
            turned_ref[...], got_ref[2 - z], preferred_element_type=F32
        )

    @pl.when(most > SEGS)
    def _():
        @pl.loop(0, tiles)
        def _(tile):
            count = (end_ref[9, group, tile] + SEGS - 1) // SEGS
            start = pl.multiple_of(jnp.minimum(tile * TILE, rows - TILE), SEG)
            row = start + lax.broadcasted_iota(jnp.int32, (TILE, 1), 0)
            fresh = row >= tile * TILE

            @pl.loop(1, count)
            def _(p):
                @pl.when(p < LISTED)
                def _():
                    for j in range(SEGS):
                        spill[j] = listed_ref[p * SEGS + j, group, tile]

                @pl.when(p >= LISTED)
                def _():
                    @pl.loop(0, SEGS)
                    def _(j):
                        slot = p * SEGS + j
                        base = jnp.int32(-1)
                        begin = jnp.int32(0)
                        for block in range(10):
                            end = end_ref[block, group, tile]
                            here = (slot >= begin) & (slot < end)
                            first = first_ref[block, group, tile]
                            base = jnp.where(here, first + slot - begin, base)
                            begin = end
                        spill[j] = base

                names, source = source_of([spill[j] for j in range(SEGS)])
                beside = feat_ref[pl.ds(start, TILE), :]
                for z in range(3):
                    col = columns[slot, pl.ds(start, TILE), z : z + 1]
                    more = pick(jnp.where(fresh, col, NOWHERE), names, source)
                    got_ref[2 - z, pl.ds(start, TILE)] += more
                    wg_ref[(2 - z) * chans : (3 - z) * chans] += lax.dot_general(
                        beside, more, (((0,), (0,)), ((), ())), preferred_element_type=F32
                    )


def gather_outer(plan, pieces, feat, turned):
    laid, listed, low, ends = plan
    rows, chans = feat.shape
    begins, *pieces = pieces
    width = pieces[1].shape[0]
    groups = laid.shape[0]
    smem = pl.BlockSpec(memory_space=pltpu.SMEM)
    return pl.pallas_call(
        functools.partial(gather_kernel, rows, width),
        grid=(groups,),
        out_shape=(
            jax.ShapeDtypeStruct((3 * groups, rows, chans), BF),
            jax.ShapeDtypeStruct((3 * groups * chans, chans), F32),
        ),
        in_specs=[smem] * 4
        + [pl.BlockSpec(laid.shape, lambda g: (0, 0, 0))]
        + [pl.BlockSpec(memory_space=pl.ANY)] * 7
        + [
            pl.BlockSpec((chans, rows), lambda g: (0, 0)),
            pl.BlockSpec((rows, chans), lambda g: (0, 0)),
        ],
        out_specs=(
            pl.BlockSpec((3, rows, chans), lambda g: (groups - 1 - g, 0, 0)),
            pl.BlockSpec((3 * chans, chans), lambda g: (groups - 1 - g, 0)),
        ),
        scratch_shapes=[
            pltpu.VMEM((rows + 9 * width, chans), BF),
            pltpu.VMEM((2, laid.shape[2], laid.shape[1]), jnp.int32),
            pltpu.SMEM((SEGS,), jnp.int32),
            pltpu.SemaphoreType.DMA((10,)),
        ],
        compiler_params=pltpu.CompilerParams(vmem_limit_bytes=56 << 20),
        cost_estimate=pl.CostEstimate(
            flops=12 * groups * rows * chans * chans,
            bytes_accessed=6 * groups * rows * chans,
            transcendentals=0,
        ),
    )(listed, low, ends, begins, laid, *pieces, turned, feat)


def back_kernel(*refs):
    gots, w_ref, out_ref = refs[:-2], refs[-2], refs[-1]
    got = [ref[k] for ref in gots for k in range(ref.shape[0])]
    total = lax.dot_general(
        jnp.concatenate(got, axis=1),
        jnp.concatenate([w_ref[k] for k in range(len(got))], axis=1),
        (((1,), (1,)), ((), ())),
        preferred_element_type=F32,
    )
    out_ref[...] = total.astype(BF)


def back_products(got, weight, first, last):
    offsets, chans, _ = weight.shape
    count = last - first
    block = 256 if count % 256 == 0 else count
    return pl.pallas_call(
        back_kernel,
        grid=(count // block,),
        out_shape=jax.ShapeDtypeStruct((count, chans), BF),
        in_specs=[
            pl.BlockSpec(
                (offsets // PARTS, block, chans),
                lambda i, part=part: (part, i + first // block, 0),
            )
            for part in range(PARTS)
        ]
        + [pl.BlockSpec(weight.shape, lambda i: (0, 0, 0))],
        out_specs=pl.BlockSpec((block, chans), lambda i: (i, 0)),
        compiler_params=pltpu.CompilerParams(vmem_limit_bytes=40 << 20),
        cost_estimate=pl.CostEstimate(
            flops=2 * offsets * count * chans * chans,
            bytes_accessed=2 * offsets * count * chans,
            transcendentals=0,
        ),
    )(*[got] * PARTS, weight)


def window_of(used, width):
    part = -(-(width // 2) // SEG) * SEG
    return part, -(-jnp.maximum(used - part, 0) // SEG) * SEG


def table_pieces(own, border, used_by):
    rows, width = own.shape[0], border.shape[0]
    size_x, size_y = lax.axis_size("gx"), lax.axis_size("gy")
    at_x, at_y = lax.axis_index("gx"), lax.axis_index("gy")
    part, start = window_of(jnp.sum((border < rows).astype(jnp.int32)), width)
    below = (at_x - 1) * size_y + at_y + jnp.arange(-1, 2)
    below = jnp.clip(below, 0, size_x * size_y - 1)
    _, begins = window_of(used_by[below], width)
    begins = jnp.concatenate([begins, jnp.zeros((6,), jnp.int32)])
    edge = jnp.take(own, border, axis=0, mode="clip")
    upper = lax.dynamic_slice_in_dim(edge, start, part, axis=0)
    pair = jnp.stack(shift(upper, edge[:part], "gx"))
    low, high = shift(edge, edge, "gy")
    low_pair, high_pair = shift(pair, pair, "gy")
    return begins, own, edge, low, high, pair, low_pair, high_pair


def step(features, pre_norm, out_grad, weight, gamma, beta, neighbors, boundary, counts):
    feat = features[0, 0]
    rows, chans = feat.shape
    border = boundary[0, 0]
    links = neighbors[0, 0]
    width = border.shape[0]
    tiles = -(-rows // TILE)
    plan = plan_segments(links, rows, width, tiles)
    turned = feat.T
    live = (lax.iota(jnp.int32, rows) < counts[0, 0])[:, None]
    zval = pre_norm[0, 0].astype(F32)
    zlive = jnp.where(live, zval, F32(0.0))
    own = jnp.stack(
        [
            jnp.sum(zlive, axis=0),
            jnp.sum(zlive * zval, axis=0),
            jnp.broadcast_to(counts[0, 0].astype(F32), (chans,)),
            jnp.broadcast_to(jnp.sum((border < rows).astype(F32)), (chans,)),
        ]
    )
    every = from_everyone(own)
    sums = jnp.sum(every, axis=0)
    count = sums[2]
    mean = sums[0] / count
    var = sums[1] / count - mean * mean
    rstd = lax.rsqrt(var + 1e-05)
    zhat = (zval - mean) * rstd
    act = gamma * zhat + beta
    sig = jax.nn.sigmoid(act)
    grad_act = jnp.where(
        live, out_grad[0, 0].astype(F32) * sig * (1.0 + act * (1.0 - sig)), F32(0.0)
    )
    pair = jnp.stack([jnp.sum(grad_act, axis=0), jnp.sum(grad_act * zhat, axis=0)])
    grads = jnp.sum(from_everyone(pair), axis=0)
    beta_grad, gamma_grad = grads[0], grads[1]
    dz = jnp.where(
        live,
        gamma * rstd * (grad_act - beta_grad / count - zhat * gamma_grad / count),
        F32(0.0),
    ).astype(BF)
    pieces = table_pieces(dz, border, every[:, 3, 0].astype(jnp.int32))
    near, wgrad = gather_outer(plan, pieces, feat, turned)
    weight_grad = scatter_sum(wgrad)
    cut = rows // 4 * 3
    in_grad = [back_products(near, weight, 0, cut)]
    in_grad.append(back_products(near, weight, cut, rows))
    in_grad = jnp.concatenate(in_grad)
    return (in_grad[None, None], weight_grad.reshape(-1, chans), gamma_grad, beta_grad)


def solution(mesh):
    placed = (
        P("gx", "gy", None, None),
        P("gx", "gy", None, None),
        P("gx", "gy", None, None),
        P(),
        P(),
        P(),
        P("gx", "gy", None, None),
        P("gx", "gy", None),
        P("gx", "gy"),
    )
    return jax.shard_map(
        step,
        mesh=mesh,
        in_specs=placed,
        out_specs=(P("gx", "gy", None, None), P(("gx", "gy"), None), P(), P()),
        check_vma=False,
    )
```
